32 devices in a mesh: section: 4 (over z), dp: 8 (over y, x, core).
Axes of the slice: x: 2, y: 2, z: 4, core: 2. Of those that a mesh axis runs over, the one named last changes fastest.
Arguments:
- tokens: bfloat16 [64, 32, 3584], P('dp'), may hold values from -6 to 6
- lengths: int32 [64], P('dp'), may hold values from 1 to 32
- assign: int32 [64, 2], P('dp'), may hold values from 0 to 7, as said below
- group_ids: int32 [64], P('dp'), may hold values from 0 to 7
- rewards: float32 [64], P('dp'), may hold values from -6 to 6
- norm_gain: bfloat16 [4, 3584], P('section'), may hold values from 0.5 to 1.5
- w_query: bfloat16 [4, 3584, 1792], P('section', 'dp'), may hold values from -0.09375 to 0.09375
- w_keyval: bfloat16 [4, 3584, 512], P('section', 'dp'), may hold values from -0.09375 to 0.09375
- w_out: bfloat16 [4, 1792, 3584], P('section', 'dp'), may hold values from -0.125 to 0.125
Outputs:
- hidden: bfloat16 [16, 128, 3584], P('dp', None, 'section')
- token_adv: bfloat16 [16, 128], P('dp')
The draws below stay inside these ranges and needn't reach their ends.
Inputs may be any that keep to these rules, and one draw needn't show every extreme that they name: assign[g,0] is one of the 4 dp indices from the sequence's own upward, wrapping; each dp index sends exactly 2 sequences to each of them; assign[g,1] is a row of the owner, and every row of every owner receives exactly 4 sequences.
All inputs are finite; a program needn't handle non-finite values.
Results may differ from the reference program's by a relative error of at most 0.014.
Values may be sent and summed in bfloat16 or wider, within the bound.
A program may use at most 128 MiB of HBM per device.

```python
import math
import jax
import jax.numpy as jnp
from jax import lax

D = 3584
HEADS = 14
KV_HEADS = 2
HEAD = 128
ROW = 128
SEQ_ROW = 4
ROWS_DEV = 2
SEQ_DEV = 8
CAP = 2
LMAX = 32
SEQ_TOT = 64
GROUPS = 8
N_SECTION = 4
N_DP = 8


def draw_assign(key, part):
    sources = SEQ_TOT // SEQ_DEV
    keys_src = jax.random.split(jax.random.fold_in(key, 11), sources)
    send_perm = jax.vmap(lambda one_key: jax.random.permutation(one_key, SEQ_DEV))(keys_src).astype(jnp.int32)
    reach = send_perm // CAP
    source_ids = jnp.arange(sources, dtype=jnp.int32)[:, None]
    owners = (source_ids + reach) % sources
    keys_own = jax.random.split(jax.random.fold_in(key, 12), sources)
    row_perm = jax.vmap(lambda one_key: jax.random.permutation(one_key, SEQ_DEV))(keys_own).astype(jnp.int32)
    target_row = row_perm[owners, send_perm] // SEQ_ROW
    return jnp.stack([owners, target_row], -1).reshape(SEQ_TOT, 2).astype(jnp.int32)


def plant(array, stream_key, least, largest):
    longest = array.shape.index(max(array.shape))
    spots = []
    for shift in (0, 1):
        where = [jax.random.randint(jax.random.fold_in(stream_key, axis), (), 0, length) for axis, length in enumerate(array.shape)]
        where[longest] = (where[longest] + shift) % array.shape[longest]
        spots.append(tuple(where))
    return array.at[spots[0]].set(least).at[spots[1]].set(largest)


def levels(key, extent, shards, least, high):
    def one(dim, parts):
        heights = jax.random.uniform(jax.random.fold_in(jax.random.fold_in(key, 6), dim), (parts,), jnp.float32, least / len(shards), high / len(shards))
        return jnp.repeat(jnp.exp(heights), extent[dim] // parts).reshape((-1,) + (1,) * (len(extent) - dim - 1))

    gain = one(*shards[0])
    for cut in shards[1:]:
        gain = gain * one(*cut)
    return gain


def gaussian(stream_key, extent, deviation, most, cuts=(), kind=jnp.bfloat16):
    drawn = deviation * jax.random.normal(stream_key, extent, jnp.float32)
    if cuts:
        drawn = drawn * levels(stream_key, extent, cuts, -0.22, 0.18)
    return jnp.clip(drawn, -most, most).astype(kind)


def setup_inputs(seed: int = 0) -> dict:
    streams_of = jax.random.split(jax.random.key(seed), 10)
    return {
        "tokens": gaussian(streams_of[0], (SEQ_TOT, LMAX, D), 1.0, 6.0, ((0, 8),)),
        "lengths": plant(jax.random.randint(streams_of[1], (SEQ_TOT,), 1, LMAX + 1), jax.random.fold_in(streams_of[1], 1), 1, LMAX).astype(jnp.int32),
        "assign": draw_assign(jax.random.fold_in(streams_of[9], 71), 0),
        "group_ids": plant(jax.random.randint(streams_of[3], (SEQ_TOT,), 0, GROUPS), jax.random.fold_in(streams_of[3], 1), 0, GROUPS - 1).astype(jnp.int32),
        "rewards": gaussian(streams_of[4], (SEQ_TOT,), 1.0, 6.0, ((0, 8),), jnp.float32),
        "norm_gain": jnp.clip(1.0 + 0.1 * jax.random.normal(streams_of[5], (N_SECTION, D), jnp.float32), 0.5, 1.5).astype(jnp.bfloat16),
        "w_query": gaussian(streams_of[6], (N_SECTION, D, HEADS * HEAD), D ** -0.5, 0.09375, ((0, 4), (1, 8))),
        "w_keyval": gaussian(streams_of[7], (N_SECTION, D, 2 * KV_HEADS * HEAD), D ** -0.5, 0.09375, ((0, 4), (1, 8))),
        "w_out": gaussian(streams_of[8], (N_SECTION, HEADS * HEAD, D), (HEADS * HEAD) ** -0.5, 0.125, ((0, 4), (1, 8))),
    }


EPS = 1e-06
THETA = 1000000.0

def rotate(inputs, position):
    half_size = inputs.shape[-1] // 2
    inverse = THETA ** (-(jnp.arange(half_size, dtype=jnp.float32) * 2.0 / inputs.shape[-1]))
    angles = position.astype(jnp.float32)[..., None] * inverse
    cosine = jnp.cos(angles)[:, :, None, :]
    sine_part = jnp.sin(angles)[:, :, None, :]
    first_half = inputs[..., :half_size]
    second = inputs[..., half_size:]
    return jnp.concatenate([first_half * cosine - second * sine_part, second * cosine + first_half * sine_part], -1)

def attend_block(rows_in, segment, position, gain_row, query_full, keyval_full, out_full):
    count, row_len, width = rows_in.shape
    wide_in = rows_in.astype(jnp.float32)
    variance = lax.optimization_barrier(jnp.mean(wide_in * wide_in, -1, keepdims=True))
    normed = (wide_in * lax.rsqrt(variance + EPS) * gain_row.astype(jnp.float32)).astype(jnp.bfloat16)
    normed = normed.reshape(count * row_len, width)
    head_count = query_full.shape[1] // HEAD
    kv_count = keyval_full.shape[1] // (2 * HEAD)
    per_group = head_count // kv_count
    queries = jnp.dot(normed, query_full, preferred_element_type=jnp.float32).reshape(count, row_len, head_count, HEAD)
    queries = rotate(queries, position).astype(jnp.bfloat16)
    keyval = jnp.dot(normed, keyval_full, preferred_element_type=jnp.float32).reshape(count, row_len, 2, kv_count, HEAD)
    key_rows = rotate(keyval[:, :, 0], position).astype(jnp.bfloat16)
    value_rows = keyval[:, :, 1].astype(jnp.bfloat16)
    grouped = queries.reshape(count, row_len, kv_count, per_group, HEAD)
    scores = jnp.einsum('nqkgd,nskd->nkgqs', grouped.astype(jnp.float32), key_rows.astype(jnp.float32)) / math.sqrt(HEAD)
    columns = jnp.arange(row_len)
    allowed = (segment[:, :, None] == segment[:, None, :]) & (columns[None, None, :] <= columns[None, :, None])
    scores = jnp.where(allowed[:, None, None], scores, -1e+30)
    top_score = lax.optimization_barrier(jnp.max(scores, -1, keepdims=True))
    expo = jnp.exp(scores - top_score)
    weights = (expo / lax.optimization_barrier(jnp.sum(expo, -1, keepdims=True))).astype(jnp.bfloat16)
    mixed_heads = jnp.einsum('nkgqs,nskd->nqkgd', weights.astype(jnp.float32), value_rows.astype(jnp.float32))
    mixed_heads = mixed_heads.astype(jnp.bfloat16).reshape(count * row_len, head_count * HEAD)
    updated = wide_in + jnp.dot(mixed_heads, out_full, preferred_element_type=jnp.float32).reshape(count, row_len, width)
    return updated.astype(jnp.bfloat16)

def reference(tokens, lengths, assign, group_ids, rewards, norm_gain, w_query, w_keyval, w_out):
    total_rows = N_DP * ROWS_DEV
    packed_row = assign[:, 0] * ROWS_DEV + assign[:, 1]
    onehot = (packed_row[:, None] == jnp.arange(total_rows, dtype=jnp.int32)[None, :]).astype(jnp.int32)
    fill = onehot * lengths[:, None]
    running = jnp.cumsum(fill, 0) - fill
    offset = lax.optimization_barrier(jnp.sum(running * onehot, 1)).astype(jnp.int32)
    group_sums = jax.ops.segment_sum(rewards, group_ids, GROUPS)
    counts = jax.ops.segment_sum(jnp.ones_like(rewards), group_ids, GROUPS)
    group_mean = group_sums / jnp.maximum(counts, 1.0)
    adv = (rewards - group_mean[group_ids]).astype(jnp.bfloat16)
    inside_at = jnp.arange(LMAX, dtype=jnp.int32)
    target = packed_row[:, None] * ROW + offset[:, None] + inside_at[None, :]
    target = jnp.where(inside_at[None, :] < lengths[:, None], target, total_rows * ROW).reshape(-1)
    width = tokens.shape[2]
    packed = jnp.zeros((total_rows * ROW, width), jnp.bfloat16).at[target].set(tokens.reshape(-1, width), mode='drop')
    seq_ids = jnp.broadcast_to(jnp.arange(SEQ_TOT, dtype=jnp.int32)[:, None], (SEQ_TOT, LMAX)).reshape(-1)
    segment = jnp.full((total_rows * ROW,), -1, jnp.int32).at[target].set(seq_ids, mode='drop')
    position = jnp.zeros((total_rows * ROW,), jnp.int32).at[target].set(jnp.broadcast_to(inside_at[None, :], (SEQ_TOT, LMAX)).reshape(-1), mode='drop')
    token_adv = jnp.zeros((total_rows * ROW,), jnp.bfloat16).at[target].set(jnp.broadcast_to(adv[:, None], (SEQ_TOT, LMAX)).reshape(-1), mode='drop')
    rows_now = packed.reshape(total_rows, ROW, width)
    segment = segment.reshape(total_rows, ROW)
    position = position.reshape(total_rows, ROW)
    for section_id in range(N_SECTION):
        rows_now = attend_block(rows_now, segment, position, norm_gain[section_id], w_query[section_id], w_keyval[section_id], w_out[section_id])
    return (rows_now, token_adv.reshape(total_rows, ROW))
```

```python
import functools
import math

import jax
import jax.numpy as jnp
from jax import lax
from jax.experimental import pallas as pl
from jax.experimental.pallas import tpu as pltpu
from jax.sharding import PartitionSpec as P

HEAD = 128
ROW = 128
SPREAD = 4
GROUP_AVG = 8
ROWS_DEV = 2
CAP = 2


EPS = 1e-06
THETA = 1000000.0


def from_behind(block, axis, distance):
    devices = range(lax.axis_size(axis))
    route = [((i - distance) % len(devices), i) for i in devices]
    return lax.ppermute(block, axis, route)


def shifted(shard, axis, by):
    length = lax.axis_size(axis)
    pairs = [(i, i + by) for i in range(length) if 0 <= i + by < length]
    return lax.ppermute(shard, axis, pairs)


CORES = 2
MESH = pl.DeviceIdType.MESH


def chip_ring(chips):
    side = math.isqrt(chips)
    while chips % side:
        side -= 1
    tall, wide = chips // side, side
    if wide == 1:
        return list(range(chips))
    walk = []
    for y in range(tall):
        across = range(1, wide) if y % 2 == 0 else range(wide - 1, 0, -1)
        walk += [y * wide + x for x in across]
    return walk + [y * wide for y in range(tall - 1, -1, -1)]


def look(table, index):
    found = jnp.int32(0)
    for at, entry in enumerate(table):
        found = found + jnp.where(index == at, jnp.int32(entry), jnp.int32(0))
    return found


def gather_kernel(devices, ins_outs, *refs):
    count = ins_outs
    shards, facts = refs[:count], refs[count]
    wholes, all_facts = refs[count + 1 : 2 * count + 1], refs[2 * count + 1]
    rest = refs[2 * count + 2 :]
    stages, stage_facts = rest[:count], rest[count]
    (local_in, local_out, ring_send, ring_recv, pair_send, pair_recv, fact_send, fact_recv) = rest[
        count + 1 :
    ]
    me = lax.axis_index("dp")
    chips = devices // CORES
    core = lax.rem(me, CORES)
    chip = me // CORES
    partner = me + 1 - 2 * core
    walk = chip_ring(chips)
    place_of = [walk.index(c) for c in range(chips)]
    place = look(place_of, chip)

    def at_place(offset):
        return look(walk, lax.rem(place + offset + 2 * chips, chips)) * CORES + core

    near = (at_place(1), at_place(-1))

    barrier = pltpu.get_barrier_semaphore()
    for step in range(1, devices):
        other = lax.rem(me + step, devices)
        pl.semaphore_signal(barrier, inc=1, device_id={"dp": other}, device_id_type=MESH)
    pl.semaphore_wait(barrier, devices - 1)

    def piece(ref, slot, way):
        half = ref.shape[-1] // 2
        return ref.at[slot, :, pl.ds(way * half, half)]

    def ring_copy(k, way, step, origin):
        source = piece(shards[k], 0, way) if step == 0 else piece(wholes[k], origin, way)
        return pltpu.make_async_remote_copy(
            src_ref=source,
            dst_ref=piece(wholes[k], origin, way),
            send_sem=ring_send.at[k, way, step],
            recv_sem=ring_recv.at[k, way, step],
            device_id={"dp": near[way]},
            device_id_type=MESH,
        )

    def pair_copy(k, way, step, source, slot):
        return pltpu.make_async_remote_copy(
            src_ref=source,
            dst_ref=piece(wholes[k], slot, way),
            send_sem=pair_send.at[k, way, step],
            recv_sem=pair_recv.at[k, way, step],
            device_id={"dp": partner},
            device_id_type=MESH,
        )

    sent = []
    for step in range(1, devices):
        copy = pltpu.make_async_remote_copy(
            src_ref=facts.at[0],
            dst_ref=all_facts.at[me],
            send_sem=fact_send.at[step],
            recv_sem=fact_recv.at[step],
            device_id={"dp": lax.rem(me + step, devices)},
            device_id_type=MESH,
        )
        copy.start()
        sent.append(copy)
    for k in range(count):
        for way in range(2):
            copy = ring_copy(k, way, 0, me)
            copy.start()
            sent.append(copy)
    loads = []
    for k, (source, stage) in enumerate(zip(shards + (facts,), stages + (stage_facts,))):
        load = pltpu.make_async_copy(source, stage, local_in.at[k])
        load.start()
        loads.append(load)
    for k in range(count):
        for way in range(2):
            copy = pair_copy(k, way, 0, piece(shards[k], 0, way), me)
            copy.start()
            sent.append(copy)
    stores = []
    for k, (stage, whole) in enumerate(zip(stages + (stage_facts,), wholes + (all_facts,))):
        loads[k].wait()
        store = pltpu.make_async_copy(stage, whole.at[pl.ds(me, 1)], local_out.at[k])
        store.start()
        stores.append(store)
    for step in range(chips - 1):
        for k in range(count):
            for way in range(2):
                sign = -1 if way == 0 else 1
                origin = at_place(sign * (step + 1))
                ring_copy(k, way, step, origin).wait_recv()
                if step < chips - 2:
                    copy = ring_copy(k, way, step + 1, origin)
                    copy.start()
                    sent.append(copy)
                copy = pair_copy(k, way, step + 1, piece(wholes[k], origin, way), origin)
                copy.start()
                sent.append(copy)
    for step in range(chips):
        for k in range(count):
            for way in range(2):
                sign = -1 if way == 0 else 1
                slot = at_place(sign * step) + 1 - 2 * core
                pair_copy(k, way, step, piece(wholes[k], slot, way), slot).wait_recv()
    for step in range(1, devices):
        slot = lax.rem(me - step + devices, devices)
        pltpu.make_async_remote_copy(
            src_ref=facts.at[0],
            dst_ref=all_facts.at[slot],
            send_sem=fact_send.at[step],
            recv_sem=fact_recv.at[step],
            device_id={"dp": slot},
            device_id_type=MESH,
        ).wait_recv()
    for copy in sent:
        copy.wait_send()
    for store in stores:
        store.wait()


def gather_all(weights, facts):
    devices = lax.axis_size("dp")
    count = len(weights)
    chips = devices // CORES
    arrays = tuple(weights) + (facts,)
    sent = sum(w.size * w.dtype.itemsize for w in weights)
    dma = pltpu.SemaphoreType.DMA
    return pl.pallas_call(
        functools.partial(gather_kernel, devices, count),
        out_shape=tuple(
            jax.ShapeDtypeStruct((devices,) + w.shape[1:], w.dtype) for w in arrays
        ),
        in_specs=[pl.BlockSpec(memory_space=pl.ANY)] * (count + 1),
        out_specs=tuple(pl.BlockSpec(memory_space=pl.ANY) for _ in arrays),
        scratch_shapes=[pltpu.VMEM(w.shape, w.dtype) for w in arrays]
        + [
            dma((count + 1,)),
            dma((count + 1,)),
            dma((count, 2, chips)),
            dma((count, 2, chips)),
            dma((count, 2, chips)),
            dma((count, 2, chips)),
            dma((devices,)),
            dma((devices,)),
        ],
        compiler_params=pltpu.CompilerParams(collective_id=0, has_side_effects=True),
        cost_estimate=pl.CostEstimate(
            flops=0, bytes_accessed=4 * devices * sent, transcendentals=0
        ),
    )(*arrays)


def rotate(inputs, position):
    half_size = inputs.shape[-1] // 2
    inverse = THETA ** (-(jnp.arange(half_size, dtype=jnp.float32) * 2.0 / inputs.shape[-1]))
    angles = position.astype(jnp.float32)[..., None] * inverse
    cosine = jnp.cos(angles)[:, :, None, :]
    sine_part = jnp.sin(angles)[:, :, None, :]
    first_half = inputs[..., :half_size]
    second = inputs[..., half_size:]
    return jnp.concatenate(
        [first_half * cosine - second * sine_part, second * cosine + first_half * sine_part], -1
    )


def attend_block(rows_in, segment, position, gain_row, query_full, keyval_full, out_full):
    count, row_len, width = rows_in.shape
    wide_in = rows_in.astype(jnp.float32)
    variance = jnp.mean(wide_in * wide_in, -1, keepdims=True)
    normed = (wide_in * lax.rsqrt(variance + EPS) * gain_row.astype(jnp.float32)).astype(
        jnp.bfloat16
    )
    normed = normed.reshape(count * row_len, width)
    head_count = query_full.shape[1] // HEAD
    kv_count = keyval_full.shape[1] // (2 * HEAD)
    per_group = head_count // kv_count
    queries = jnp.dot(normed, query_full, preferred_element_type=jnp.float32).reshape(
        count, row_len, head_count, HEAD
    )
    queries = rotate(queries, position).astype(jnp.bfloat16)
    keyval = jnp.dot(normed, keyval_full, preferred_element_type=jnp.float32).reshape(
        count, row_len, 2, kv_count, HEAD
    )
    key_rows = rotate(keyval[:, :, 0], position).astype(jnp.bfloat16)
    value_rows = keyval[:, :, 1].astype(jnp.bfloat16)
    grouped = queries.reshape(count, row_len, kv_count, per_group, HEAD)
    scores = jnp.einsum(
        "nqkgd,nskd->nkgqs", grouped, key_rows, preferred_element_type=jnp.float32
    ) / math.sqrt(HEAD)
    columns = jnp.arange(row_len)
    allowed = (segment[:, :, None] == segment[:, None, :]) & (
        columns[None, None, :] <= columns[None, :, None]
    )
    scores = jnp.where(allowed[:, None, None], scores, -1e30)
    top_score = jnp.max(scores, -1, keepdims=True)
    expo = jnp.exp(scores - top_score)
    weights = (expo / jnp.sum(expo, -1, keepdims=True)).astype(jnp.bfloat16)
    mixed_heads = jnp.einsum(
        "nkgqs,nskd->nqkgd", weights, value_rows, preferred_element_type=jnp.float32
    )
    mixed_heads = mixed_heads.astype(jnp.bfloat16).reshape(count * row_len, head_count * HEAD)
    updated = wide_in + jnp.dot(mixed_heads, out_full, preferred_element_type=jnp.float32).reshape(
        count, row_len, width
    )
    return updated.astype(jnp.bfloat16)


def body(tokens, lengths, assign, group_ids, rewards, norm_gain, w_query, w_keyval, w_out):
    seq_dev, lmax_len, width = tokens.shape
    dp_count = lax.axis_size("dp")
    sections = lax.axis_size("section")
    dp_index = lax.axis_index("dp")
    section_me = lax.axis_index("section")
    rows_dev = ROWS_DEV
    groups_all = seq_dev * dp_count // GROUP_AVG
    owners = assign[:, 0]
    reach = (owners - dp_index) % dp_count
    local_ids = jnp.arange(seq_dev, dtype=jnp.int32)
    earlier = local_ids[None, :] < local_ids[:, None]
    rank_in = jnp.sum(((reach[:, None] == reach[None, :]) & earlier).astype(jnp.int32), 1)
    slot_ids = reach * CAP + rank_in
    picked = (slot_ids[None, :] == local_ids[:, None]).astype(jnp.int32)
    send_tok = tokens[jnp.sum(picked * local_ids[None, :], 1)]
    got_tok = []
    for reach_step in range(SPREAD):
        tok_piece = send_tok[reach_step * CAP : (reach_step + 1) * CAP]
        if reach_step > 0:
            tok_piece = from_behind(tok_piece, "dp", reach_step)
        got_tok.append(tok_piece)
    recv_tok = jnp.concatenate(got_tok, 0)
    facts = jnp.stack(
        [
            (owners * rows_dev + assign[:, 1]).astype(jnp.float32),
            lengths.astype(jnp.float32),
            group_ids.astype(jnp.float32),
            rewards,
            slot_ids.astype(jnp.float32),
        ]
    )
    facts = jnp.pad(facts, ((0, 8 - facts.shape[0]), (0, 128 - seq_dev)))[None]
    query_full, keyval_full, out_full, all_facts = gather_all((w_query, w_keyval, w_out), facts)
    query_full = query_full.reshape(-1, query_full.shape[-1])
    keyval_full = keyval_full.reshape(-1, keyval_full.shape[-1])
    out_full = out_full.reshape(-1, out_full.shape[-1])
    known = all_facts[:, :, :seq_dev].transpose(1, 0, 2).reshape(8, dp_count * seq_dev)
    seq_row = known[0].astype(jnp.int32)
    seq_len = known[1].astype(jnp.int32)
    seq_group = known[2].astype(jnp.int32)
    seq_slot = known[4].astype(jnp.int32)
    all_ids = jnp.arange(dp_count * seq_dev, dtype=jnp.int32)
    before = (seq_row[:, None] == seq_row[None, :]) & (all_ids[:, None] < all_ids[None, :])
    seq_off = jnp.sum(jnp.where(before, seq_len[:, None], 0), 0)
    member = (seq_group[None, :] == jnp.arange(groups_all, dtype=jnp.int32)[:, None]).astype(
        jnp.float32
    )
    group_mean = jnp.sum(member * known[3][None, :], 1) / jnp.maximum(jnp.sum(member, 1), 1.0)
    adv = (known[3] - jnp.sum(member * group_mean[:, None], 0)).astype(jnp.bfloat16)
    cell_ids = jnp.arange(rows_dev * ROW, dtype=jnp.int32)
    cell_row = dp_index * rows_dev + cell_ids // ROW
    inside_at = (cell_ids % ROW)[None, :] - seq_off[:, None]
    matched = (
        (seq_row[:, None] == cell_row[None, :])
        & (inside_at >= 0)
        & (inside_at < seq_len[:, None])
    )
    matched_int = matched.astype(jnp.int32)
    filled = jnp.sum(matched_int, 0) > 0
    anchor = jnp.sum(matched_int * (seq_slot[:, None] * lmax_len + inside_at), 0)
    flat_tok = recv_tok.reshape(seq_dev * lmax_len, width)
    packed = jnp.where(filled[:, None], flat_tok[anchor], jnp.zeros((), jnp.bfloat16)).reshape(
        rows_dev, ROW, width
    )
    segment = jnp.where(filled, jnp.sum(matched_int * all_ids[:, None], 0), -1).reshape(
        rows_dev, ROW
    )
    position = jnp.sum(matched_int * inside_at, 0).reshape(rows_dev, ROW)
    token_adv = jnp.sum(matched.astype(jnp.float32) * adv.astype(jnp.float32)[:, None], 0)
    token_adv = token_adv.astype(jnp.bfloat16).reshape(rows_dev, ROW)
    gain_row = norm_gain[0]
    per_block = 1
    block_count = rows_dev // per_block
    tick_count = block_count + sections - 1
    share = width // sections
    last = sections - 1
    outputs = []
    result_rows = jnp.zeros((per_block, ROW, width), jnp.bfloat16)
    carried = result_rows
    for tick_index in range(tick_count):
        if tick_index > 0:
            carried = shifted(result_rows, "section", 1)
        if tick_index < block_count:
            fresh_rows = packed[tick_index * per_block : (tick_index + 1) * per_block]
        else:
            fresh_rows = jnp.zeros_like(carried)
        current_rows = jnp.where(section_me == 0, fresh_rows, carried)
        block_now = tick_index - section_me
        block_at = jnp.clip(block_now, 0, block_count - 1)
        segment_b = lax.dynamic_slice_in_dim(segment, block_at * per_block, per_block, 0)
        position_b = lax.dynamic_slice_in_dim(position, block_at * per_block, per_block, 0)
        result_rows = attend_block(
            current_rows, segment_b, position_b, gain_row, query_full, keyval_full, out_full
        )
        done_at = tick_index - (sections - 1)
        if done_at >= 0 and done_at < block_count:
            kept = result_rows[:, :, last * share :]
            for target in range(last):
                part = result_rows[:, :, target * share : (target + 1) * share]
                part = lax.ppermute(part, "section", [(last, target)])
                kept = jnp.where(section_me == target, part, kept)
            outputs.append(kept)
    hidden = jnp.concatenate(outputs, 0)
    return (hidden, token_adv)


def solution(mesh):
    placed = (
        P("dp", None, None),
        P("dp"),
        P("dp", None),
        P("dp"),
        P("dp"),
        P("section", None),
        P("section", "dp", None),
        P("section", "dp", None),
        P("section", "dp", None),
    )
    return jax.shard_map(
        body,
        mesh=mesh,
        in_specs=placed,
        out_specs=(P("dp", None, "section"), P("dp", None)),
        check_vma=False,
    )
```

```python
import functools
import math

import jax
import jax.numpy as jnp
from jax import lax
from jax.experimental import pallas as pl
from jax.experimental.pallas import tpu as pltpu
from jax.sharding import PartitionSpec as P

HEAD = 128
ROW = 128
SPREAD = 4
GROUP_AVG = 8
ROWS_DEV = 2
CAP = 2


EPS = 1e-06
THETA = 1000000.0


def from_behind(block, axis, distance):
    devices = range(lax.axis_size(axis))
    route = [((i - distance) % len(devices), i) for i in devices]
    return lax.ppermute(block, axis, route)


def shifted(shard, axis, by):
    length = lax.axis_size(axis)
    pairs = [(i, i + by) for i in range(length) if 0 <= i + by < length]
    return lax.ppermute(shard, axis, pairs)


CORES = 2
MESH = pl.DeviceIdType.MESH


def chip_ring(chips):
    side = math.isqrt(chips)
    while chips % side:
        side -= 1
    tall, wide = chips // side, side
    if wide == 1:
        return list(range(chips))
    walk = []
    for y in range(tall):
        across = range(1, wide) if y % 2 == 0 else range(wide - 1, 0, -1)
        walk += [y * wide + x for x in across]
    return walk + [y * wide for y in range(tall - 1, -1, -1)]


def look(table, index):
    found = jnp.int32(0)
    for at, entry in enumerate(table):
        found = found + jnp.where(index == at, jnp.int32(entry), jnp.int32(0))
    return found


def gather_kernel(devices, ins_outs, *refs):
    count = ins_outs
    shards, facts = refs[:count], refs[count]
    wholes, all_facts = refs[count + 1 : 2 * count + 1], refs[2 * count + 1]
    rest = refs[2 * count + 2 :]
    stages, stage_facts = rest[:count], rest[count]
    (local_in, local_out, ring_send, ring_recv, pair_send, pair_recv, fact_send, fact_recv) = rest[
        count + 1 :
    ]
    me = lax.axis_index("dp")
    chips = devices // CORES
    core = lax.rem(me, CORES)
    chip = me // CORES
    partner = me + 1 - 2 * core
    walk = chip_ring(chips)
    place_of = [walk.index(c) for c in range(chips)]
    place = look(place_of, chip)

    def at_place(offset):
        return look(walk, lax.rem(place + offset + 2 * chips, chips)) * CORES + core

    near = (at_place(1), at_place(-1))

    barrier = pltpu.get_barrier_semaphore()
    for step in range(1, devices):
        other = lax.rem(me + step, devices)
        pl.semaphore_signal(barrier, inc=1, device_id={"dp": other}, device_id_type=MESH)
    pl.semaphore_wait(barrier, devices - 1)

    def piece(ref, slot, way):
        half = ref.shape[-1] // 2
        return ref.at[slot, :, pl.ds(way * half, half)]

    def ring_copy(k, way, step, origin):
        source = piece(shards[k], 0, way) if step == 0 else piece(wholes[k], origin, way)
        return pltpu.make_async_remote_copy(
            src_ref=source,
            dst_ref=piece(wholes[k], origin, way),
            send_sem=ring_send.at[k, way, step],
            recv_sem=ring_recv.at[k, way, step],
            device_id={"dp": near[way]},
            device_id_type=MESH,
        )

    def pair_copy(k, way, step, source, slot):
        return pltpu.make_async_remote_copy(
            src_ref=source,
            dst_ref=piece(wholes[k], slot, way),
            send_sem=pair_send.at[k, way, step],
            recv_sem=pair_recv.at[k, way, step],
            device_id={"dp": partner},
            device_id_type=MESH,
        )

    sent = []
    for step in range(1, devices):
        copy = pltpu.make_async_remote_copy(
            src_ref=facts.at[0],
            dst_ref=all_facts.at[me],
            send_sem=fact_send.at[step],
            recv_sem=fact_recv.at[step],
            device_id={"dp": lax.rem(me + step, devices)},
            device_id_type=MESH,
        )
        copy.start()
        sent.append(copy)
    for k in range(count):
        for way in range(2):
            copy = ring_copy(k, way, 0, me)
            copy.start()
            sent.append(copy)
    loads = []
    for k, (source, stage) in enumerate(zip(shards + (facts,), stages + (stage_facts,))):
        load = pltpu.make_async_copy(source, stage, local_in.at[k])
        load.start()
        loads.append(load)
    for k in range(count):
        for way in range(2):
            copy = pair_copy(k, way, 0, piece(shards[k], 0, way), me)
            copy.start()
            sent.append(copy)
    stores = []
    for k, (stage, whole) in enumerate(zip(stages + (stage_facts,), wholes + (all_facts,))):
        loads[k].wait()
        store = pltpu.make_async_copy(stage, whole.at[pl.ds(me, 1)], local_out.at[k])
        store.start()
        stores.append(store)
    for step in range(chips - 1):
        for k in range(count):
            for way in range(2):
                sign = -1 if way == 0 else 1
                origin = at_place(sign * (step + 1))
                ring_copy(k, way, step, origin).wait_recv()
                if step < chips - 2:
                    copy = ring_copy(k, way, step + 1, origin)
                    copy.start()
                    sent.append(copy)
                copy = pair_copy(k, way, step + 1, piece(wholes[k], origin, way), origin)
                copy.start()
                sent.append(copy)
    for step in range(chips):
        for k in range(count):
            for way in range(2):
                sign = -1 if way == 0 else 1
                slot = at_place(sign * step) + 1 - 2 * core
                pair_copy(k, way, step, piece(wholes[k], slot, way), slot).wait_recv()
    for step in range(1, devices):
        slot = lax.rem(me - step + devices, devices)
        pltpu.make_async_remote_copy(
            src_ref=facts.at[0],
            dst_ref=all_facts.at[slot],
            send_sem=fact_send.at[step],
            recv_sem=fact_recv.at[step],
            device_id={"dp": slot},
            device_id_type=MESH,
        ).wait_recv()
    for copy in sent:
        copy.wait_send()
    for store in stores:
        store.wait()


def gather_all(weights, facts):
    devices = lax.axis_size("dp")
    count = len(weights)
    chips = devices // CORES
    arrays = tuple(weights) + (facts,)
    sent = sum(w.size * w.dtype.itemsize for w in weights)
    dma = pltpu.SemaphoreType.DMA
    return pl.pallas_call(
        functools.partial(gather_kernel, devices, count),
        out_shape=tuple(
            jax.ShapeDtypeStruct((devices,) + w.shape[1:], w.dtype) for w in arrays
        ),
        in_specs=[pl.BlockSpec(memory_space=pl.ANY)] * (count + 1),
        out_specs=tuple(pl.BlockSpec(memory_space=pl.ANY) for _ in arrays),
        scratch_shapes=[pltpu.VMEM(w.shape, w.dtype) for w in arrays]
        + [
            dma((count + 1,)),
            dma((count + 1,)),
            dma((count, 2, chips)),
            dma((count, 2, chips)),
            dma((count, 2, chips)),
            dma((count, 2, chips)),
            dma((devices,)),
            dma((devices,)),
        ],
        compiler_params=pltpu.CompilerParams(collective_id=0, has_side_effects=True),
        cost_estimate=pl.CostEstimate(
            flops=0, bytes_accessed=4 * devices * sent, transcendentals=0
        ),
    )(*arrays)


def attend_kernel(query_ref, keyval_ref, down_ref, along_ref, cosine_ref, sine_ref, mixed_ref):
    row_len = query_ref.shape[0]
    head_count = query_ref.shape[1] // HEAD
    kv_count = keyval_ref.shape[1] // (2 * HEAD)
    per_group = head_count // kv_count
    cosine, sine = cosine_ref[...], sine_ref[...]

    def turned(part):
        return (part * cosine + pltpu.roll(part, HEAD // 2, 1) * sine).astype(jnp.bfloat16)

    rows = lax.broadcasted_iota(jnp.int32, (row_len, row_len), 0)
    columns = lax.broadcasted_iota(jnp.int32, (row_len, row_len), 1)
    allowed = (down_ref[...] == along_ref[...]) & (columns <= rows)
    for group in range(kv_count):
        keys = turned(keyval_ref[:, group * HEAD : (group + 1) * HEAD])
        values = keyval_ref[:, (kv_count + group) * HEAD : (kv_count + group + 1) * HEAD]
        values = values.astype(jnp.bfloat16)
        for head in range(group * per_group, (group + 1) * per_group):
            queries = turned(query_ref[:, head * HEAD : (head + 1) * HEAD])
            scores = lax.dot_general(
                queries, keys, (((1,), (1,)), ((), ())), preferred_element_type=jnp.float32
            ) / math.sqrt(HEAD)
            scores = jnp.where(allowed, scores, -1e30)
            expo = jnp.exp(scores - jnp.max(scores, -1, keepdims=True))
            weights = (expo / jnp.sum(expo, -1, keepdims=True)).astype(jnp.bfloat16)
            mixed = jnp.dot(weights, values, preferred_element_type=jnp.float32)
            mixed_ref[:, head * HEAD : (head + 1) * HEAD] = mixed.astype(jnp.bfloat16)


def attend_block(rows_in, segment, cosine, sine, gain_row, query_full, keyval_full, out_full):
    _, row_len, width = rows_in.shape
    wide_in = rows_in[0].astype(jnp.float32)
    variance = jnp.mean(wide_in * wide_in, -1, keepdims=True)
    normed = (wide_in * lax.rsqrt(variance + EPS) * gain_row.astype(jnp.float32)).astype(
        jnp.bfloat16
    )
    queries = jnp.dot(normed, query_full, preferred_element_type=jnp.float32)
    keyval = jnp.dot(normed, keyval_full, preferred_element_type=jnp.float32)
    mixed_heads = pl.pallas_call(
        attend_kernel,
        out_shape=jax.ShapeDtypeStruct(queries.shape, jnp.bfloat16),
        in_specs=[pl.BlockSpec(memory_space=pltpu.VMEM)] * 6,
        out_specs=pl.BlockSpec(memory_space=pltpu.VMEM),
        compiler_params=pltpu.CompilerParams(vmem_limit_bytes=16 * 1024 * 1024),
        cost_estimate=pl.CostEstimate(
            flops=4 * row_len * row_len * queries.shape[1],
            bytes_accessed=6 * queries.size,
            transcendentals=row_len * queries.size // HEAD,
        ),
    )(queries, keyval, segment.reshape(row_len, 1), segment, cosine[0], sine[0])
    updated = wide_in + jnp.dot(mixed_heads, out_full, preferred_element_type=jnp.float32)
    return updated.astype(jnp.bfloat16)[None]


def body(tokens, lengths, assign, group_ids, rewards, norm_gain, w_query, w_keyval, w_out):
    seq_dev, lmax_len, width = tokens.shape
    dp_count = lax.axis_size("dp")
    sections = lax.axis_size("section")
    dp_index = lax.axis_index("dp")
    section_me = lax.axis_index("section")
    rows_dev = ROWS_DEV
    groups_all = seq_dev * dp_count // GROUP_AVG
    owners = assign[:, 0]
    reach = (owners - dp_index) % dp_count
    local_ids = jnp.arange(seq_dev, dtype=jnp.int32)
    earlier = local_ids[None, :] < local_ids[:, None]
    rank_in = jnp.sum(((reach[:, None] == reach[None, :]) & earlier).astype(jnp.int32), 1)
    slot_ids = reach * CAP + rank_in
    picked = (slot_ids[None, :] == local_ids[:, None]).astype(jnp.int32)
    send_tok = tokens[jnp.sum(picked * local_ids[None, :], 1)]
    got_tok = []
    for reach_step in range(SPREAD):
        tok_piece = send_tok[reach_step * CAP : (reach_step + 1) * CAP]
        if reach_step > 0:
            tok_piece = from_behind(tok_piece, "dp", reach_step)
        got_tok.append(tok_piece)
    recv_tok = jnp.concatenate(got_tok, 0)
    facts = jnp.stack(
        [
            (owners * rows_dev + assign[:, 1]).astype(jnp.float32),
            lengths.astype(jnp.float32),
            group_ids.astype(jnp.float32),
            rewards,
            slot_ids.astype(jnp.float32),
        ]
    )
    facts = jnp.pad(facts, ((0, 8 - facts.shape[0]), (0, 128 - seq_dev)))[None]
    query_full, keyval_full, out_full, all_facts = gather_all((w_query, w_keyval, w_out), facts)
    query_full = query_full.reshape(-1, query_full.shape[-1])
    keyval_full = keyval_full.reshape(-1, keyval_full.shape[-1])
    out_full = out_full.reshape(-1, out_full.shape[-1])
    known = all_facts[:, :, :seq_dev].transpose(1, 0, 2).reshape(8, dp_count * seq_dev)
    seq_row = known[0].astype(jnp.int32)
    seq_len = known[1].astype(jnp.int32)
    seq_group = known[2].astype(jnp.int32)
    seq_slot = known[4].astype(jnp.int32)
    all_ids = jnp.arange(dp_count * seq_dev, dtype=jnp.int32)
    before = (seq_row[:, None] == seq_row[None, :]) & (all_ids[:, None] < all_ids[None, :])
    seq_off = jnp.sum(jnp.where(before, seq_len[:, None], 0), 0)
    member = (seq_group[None, :] == jnp.arange(groups_all, dtype=jnp.int32)[:, None]).astype(
        jnp.float32
    )
    group_mean = jnp.sum(member * known[3][None, :], 1) / jnp.maximum(jnp.sum(member, 1), 1.0)
    adv = (known[3] - jnp.sum(member * group_mean[:, None], 0)).astype(jnp.bfloat16)
    cell_ids = jnp.arange(rows_dev * ROW, dtype=jnp.int32)
    cell_row = dp_index * rows_dev + cell_ids // ROW
    inside_at = (cell_ids % ROW)[None, :] - seq_off[:, None]
    matched = (
        (seq_row[:, None] == cell_row[None, :])
        & (inside_at >= 0)
        & (inside_at < seq_len[:, None])
    )
    matched_int = matched.astype(jnp.int32)
    filled = jnp.sum(matched_int, 0) > 0
    anchor = jnp.sum(matched_int * (seq_slot[:, None] * lmax_len + inside_at), 0)
    flat_tok = recv_tok.reshape(seq_dev * lmax_len, width)
    packed = jnp.where(filled[:, None], flat_tok[anchor], jnp.zeros((), jnp.bfloat16)).reshape(
        rows_dev, ROW, width
    )
    segment = jnp.where(filled, jnp.sum(matched_int * all_ids[:, None], 0), -1).reshape(
        rows_dev, ROW
    )
    position = jnp.sum(matched_int * inside_at, 0).reshape(rows_dev, ROW)
    token_adv = jnp.sum(matched.astype(jnp.float32) * adv.astype(jnp.float32)[:, None], 0)
    token_adv = token_adv.astype(jnp.bfloat16).reshape(rows_dev, ROW)
    half = HEAD // 2
    inverse = THETA ** (-(jnp.arange(half, dtype=jnp.float32) * 2.0 / HEAD))
    angles = position.astype(jnp.float32)[..., None] * inverse
    cosine, sine = jnp.cos(angles), jnp.sin(angles)
    cosine = jnp.concatenate([cosine, cosine], -1)
    sine = jnp.concatenate([-sine, sine], -1)
    gain_row = norm_gain[0]
    per_block = 1
    block_count = rows_dev // per_block
    tick_count = block_count + sections - 1
    share = width // sections
    last = sections - 1
    outputs = []
    result_rows = jnp.zeros((per_block, ROW, width), jnp.bfloat16)
    carried = result_rows
    for tick_index in range(tick_count):
        if tick_index > 0:
            carried = shifted(result_rows, "section", 1)
        if tick_index < block_count:
            fresh_rows = packed[tick_index * per_block : (tick_index + 1) * per_block]
        else:
            fresh_rows = jnp.zeros_like(carried)
        current_rows = jnp.where(section_me == 0, fresh_rows, carried)
        block_now = tick_index - section_me
        block_at = jnp.clip(block_now, 0, block_count - 1)
        segment_b = lax.dynamic_slice_in_dim(segment, block_at * per_block, per_block, 0)
        cosine_b = lax.dynamic_slice_in_dim(cosine, block_at * per_block, per_block, 0)
        sine_b = lax.dynamic_slice_in_dim(sine, block_at * per_block, per_block, 0)
        result_rows = attend_block(
            current_rows,
            segment_b,
            cosine_b,
            sine_b,
            gain_row,
            query_full,
            keyval_full,
            out_full,
        )
        done_at = tick_index - (sections - 1)
        if done_at >= 0 and done_at < block_count:
            kept = result_rows[:, :, last * share :]
            for target in range(last):
                part = result_rows[:, :, target * share : (target + 1) * share]
                part = lax.ppermute(part, "section", [(last, target)])
                kept = jnp.where(section_me == target, part, kept)
            outputs.append(kept)
    hidden = jnp.concatenate(outputs, 0)
    return (hidden, token_adv)


def solution(mesh):
    placed = (
        P("dp", None, None),
        P("dp"),
        P("dp", None),
        P("dp"),
        P("dp"),
        P("section", None),
        P("section", "dp", None),
        P("section", "dp", None),
        P("section", "dp", None),
    )
    return jax.shard_map(
        body,
        mesh=mesh,
        in_specs=placed,
        out_specs=(P("dp", None, "section"), P("dp", None)),
        check_vma=False,
    )
```

```python
import functools
import math

import jax
import jax.numpy as jnp
from jax import lax
from jax.experimental import pallas as pl
from jax.experimental.pallas import tpu as pltpu
from jax.sharding import PartitionSpec as P

HEAD = 128
ROW = 128
SPREAD = 4
GROUP_AVG = 8
ROWS_DEV = 2
CAP = 2


EPS = 1e-06
THETA = 1000000.0


def from_behind(block, axis, distance):
    devices = range(lax.axis_size(axis))
    route = [((i - distance) % len(devices), i) for i in devices]
    return lax.ppermute(block, axis, route)


CORES = 2
MESH = pl.DeviceIdType.MESH


def chip_ring(chips):
    side = math.isqrt(chips)
    while chips % side:
        side -= 1
    tall, wide = chips // side, side
    if wide == 1:
        return list(range(chips))
    walk = []
    for y in range(tall):
        across = range(1, wide) if y % 2 == 0 else range(wide - 1, 0, -1)
        walk += [y * wide + x for x in across]
    return walk + [y * wide for y in range(tall - 1, -1, -1)]


def look(table, index):
    found = jnp.int32(0)
    for at, entry in enumerate(table):
        found = found + jnp.where(index == at, jnp.int32(entry), jnp.int32(0))
    return found


def gather_kernel(devices, ins_outs, *refs):
    count = ins_outs
    shards, facts = refs[:count], refs[count]
    wholes, all_facts = refs[count + 1 : 2 * count + 1], refs[2 * count + 1]
    rest = refs[2 * count + 2 :]
    stages, stage_facts = rest[:count], rest[count]
    (local_in, local_out, ring_send, ring_recv, pair_send, pair_recv, fact_send, fact_recv) = rest[
        count + 1 :
    ]
    me = lax.axis_index("dp")
    chips = devices // CORES
    core = lax.rem(me, CORES)
    chip = me // CORES
    partner = me + 1 - 2 * core
    walk = chip_ring(chips)
    place_of = [walk.index(c) for c in range(chips)]
    place = look(place_of, chip)

    def at_place(offset):
        return look(walk, lax.rem(place + offset + 2 * chips, chips)) * CORES + core

    near = (at_place(1), at_place(-1))

    barrier = pltpu.get_barrier_semaphore()
    for step in range(1, devices):
        other = lax.rem(me + step, devices)
        pl.semaphore_signal(barrier, inc=1, device_id={"dp": other}, device_id_type=MESH)
    pl.semaphore_wait(barrier, devices - 1)

    def piece(ref, slot, way):
        half = ref.shape[-1] // 2
        return ref.at[slot, :, pl.ds(way * half, half)]

    def ring_copy(k, way, step, origin):
        source = piece(shards[k], 0, way) if step == 0 else piece(wholes[k], origin, way)
        return pltpu.make_async_remote_copy(
            src_ref=source,
            dst_ref=piece(wholes[k], origin, way),
            send_sem=ring_send.at[k, way, step],
            recv_sem=ring_recv.at[k, way, step],
            device_id={"dp": near[way]},
            device_id_type=MESH,
        )

    def pair_copy(k, way, step, source, slot):
        return pltpu.make_async_remote_copy(
            src_ref=source,
            dst_ref=piece(wholes[k], slot, way),
            send_sem=pair_send.at[k, way, step],
            recv_sem=pair_recv.at[k, way, step],
            device_id={"dp": partner},
            device_id_type=MESH,
        )

    sent = []
    for step in range(1, devices):
        copy = pltpu.make_async_remote_copy(
            src_ref=facts.at[0],
            dst_ref=all_facts.at[me],
            send_sem=fact_send.at[step],
            recv_sem=fact_recv.at[step],
            device_id={"dp": lax.rem(me + step, devices)},
            device_id_type=MESH,
        )
        copy.start()
        sent.append(copy)
    for k in range(count):
        for way in range(2):
            copy = ring_copy(k, way, 0, me)
            copy.start()
            sent.append(copy)
    loads = []
    for k, (source, stage) in enumerate(zip(shards + (facts,), stages + (stage_facts,))):
        load = pltpu.make_async_copy(source, stage, local_in.at[k])
        load.start()
        loads.append(load)
    for k in range(count):
        for way in range(2):
            copy = pair_copy(k, way, 0, piece(shards[k], 0, way), me)
            copy.start()
            sent.append(copy)
    stores = []
    for k, (stage, whole) in enumerate(zip(stages + (stage_facts,), wholes + (all_facts,))):
        loads[k].wait()
        store = pltpu.make_async_copy(stage, whole.at[pl.ds(me, 1)], local_out.at[k])
        store.start()
        stores.append(store)
    for step in range(chips - 1):
        for k in range(count):
            for way in range(2):
                sign = -1 if way == 0 else 1
                origin = at_place(sign * (step + 1))
                ring_copy(k, way, step, origin).wait_recv()
                if step < chips - 2:
                    copy = ring_copy(k, way, step + 1, origin)
                    copy.start()
                    sent.append(copy)
                copy = pair_copy(k, way, step + 1, piece(wholes[k], origin, way), origin)
                copy.start()
                sent.append(copy)
    for step in range(chips):
        for k in range(count):
            for way in range(2):
                sign = -1 if way == 0 else 1
                slot = at_place(sign * step) + 1 - 2 * core
                pair_copy(k, way, step, piece(wholes[k], slot, way), slot).wait_recv()
    for step in range(1, devices):
        slot = lax.rem(me - step + devices, devices)
        pltpu.make_async_remote_copy(
            src_ref=facts.at[0],
            dst_ref=all_facts.at[slot],
            send_sem=fact_send.at[step],
            recv_sem=fact_recv.at[step],
            device_id={"dp": slot},
            device_id_type=MESH,
        ).wait_recv()
    for copy in sent:
        copy.wait_send()
    for store in stores:
        store.wait()


def gather_all(weights, facts):
    devices = lax.axis_size("dp")
    count = len(weights)
    chips = devices // CORES
    arrays = tuple(weights) + (facts,)
    sent = sum(w.size * w.dtype.itemsize for w in weights)
    dma = pltpu.SemaphoreType.DMA
    return pl.pallas_call(
        functools.partial(gather_kernel, devices, count),
        out_shape=tuple(
            jax.ShapeDtypeStruct((devices,) + w.shape[1:], w.dtype) for w in arrays
        ),
        in_specs=[pl.BlockSpec(memory_space=pl.ANY)] * (count + 1),
        out_specs=tuple(pl.BlockSpec(memory_space=pl.ANY) for _ in arrays),
        scratch_shapes=[pltpu.VMEM(w.shape, w.dtype) for w in arrays]
        + [
            dma((count + 1,)),
            dma((count + 1,)),
            dma((count, 2, chips)),
            dma((count, 2, chips)),
            dma((count, 2, chips)),
            dma((count, 2, chips)),
            dma((devices,)),
            dma((devices,)),
        ],
        compiler_params=pltpu.CompilerParams(collective_id=0, has_side_effects=True),
        cost_estimate=pl.CostEstimate(
            flops=0, bytes_accessed=4 * devices * sent, transcendentals=0
        ),
    )(*arrays)


def attend_kernel(query_ref, keyval_ref, down_ref, along_ref, cosine_ref, sine_ref, mixed_ref):
    row_len = query_ref.shape[0]
    head_count = query_ref.shape[1] // HEAD
    kv_count = keyval_ref.shape[1] // (2 * HEAD)
    per_group = head_count // kv_count
    cosine, sine = cosine_ref[...], sine_ref[...]

    def turned(part):
        return (part * cosine + pltpu.roll(part, HEAD // 2, 1) * sine).astype(jnp.bfloat16)

    rows = lax.broadcasted_iota(jnp.int32, (row_len, row_len), 0)
    columns = lax.broadcasted_iota(jnp.int32, (row_len, row_len), 1)
    allowed = (down_ref[...] == along_ref[...]) & (columns <= rows)
    for group in range(kv_count):
        keys = turned(keyval_ref[:, group * HEAD : (group + 1) * HEAD])
        values = keyval_ref[:, (kv_count + group) * HEAD : (kv_count + group + 1) * HEAD]
        values = values.astype(jnp.bfloat16)
        for head in range(group * per_group, (group + 1) * per_group):
            queries = turned(query_ref[:, head * HEAD : (head + 1) * HEAD])
            scores = lax.dot_general(
                queries, keys, (((1,), (1,)), ((), ())), preferred_element_type=jnp.float32
            ) / math.sqrt(HEAD)
            scores = jnp.where(allowed, scores, -1e30)
            expo = jnp.exp(scores - jnp.max(scores, -1, keepdims=True))
            weights = (expo / jnp.sum(expo, -1, keepdims=True)).astype(jnp.bfloat16)
            mixed = jnp.dot(weights, values, preferred_element_type=jnp.float32)
            mixed_ref[:, head * HEAD : (head + 1) * HEAD] = mixed.astype(jnp.bfloat16)


def attend_block(rows_in, segment, cosine, sine, gain_row, query_full, keyval_full, out_full):
    _, row_len, width = rows_in.shape
    wide_in = rows_in[0].astype(jnp.float32)
    variance = jnp.mean(wide_in * wide_in, -1, keepdims=True)
    normed = (wide_in * lax.rsqrt(variance + EPS) * gain_row.astype(jnp.float32)).astype(
        jnp.bfloat16
    )
    queries = jnp.dot(normed, query_full, preferred_element_type=jnp.float32)
    keyval = jnp.dot(normed, keyval_full, preferred_element_type=jnp.float32)
    mixed_heads = pl.pallas_call(
        attend_kernel,
        out_shape=jax.ShapeDtypeStruct(queries.shape, jnp.bfloat16),
        in_specs=[pl.BlockSpec(memory_space=pltpu.VMEM)] * 6,
        out_specs=pl.BlockSpec(memory_space=pltpu.VMEM),
        compiler_params=pltpu.CompilerParams(vmem_limit_bytes=16 * 1024 * 1024),
        cost_estimate=pl.CostEstimate(
            flops=4 * row_len * row_len * queries.shape[1],
            bytes_accessed=6 * queries.size,
            transcendentals=row_len * queries.size // HEAD,
        ),
    )(queries, keyval, segment.reshape(row_len, 1), segment, cosine[0], sine[0])
    updated = wide_in + jnp.dot(mixed_heads, out_full, preferred_element_type=jnp.float32)
    return updated.astype(jnp.bfloat16)[None]


def body(tokens, lengths, assign, group_ids, rewards, norm_gain, w_query, w_keyval, w_out):
    seq_dev, lmax_len, width = tokens.shape
    dp_count = lax.axis_size("dp")
    sections = lax.axis_size("section")
    dp_index = lax.axis_index("dp")
    section_me = lax.axis_index("section")
    rows_dev = ROWS_DEV
    groups_all = seq_dev * dp_count // GROUP_AVG
    owners = assign[:, 0]
    reach = (owners - dp_index) % dp_count
    local_ids = jnp.arange(seq_dev, dtype=jnp.int32)
    earlier = local_ids[None, :] < local_ids[:, None]
    rank_in = jnp.sum(((reach[:, None] == reach[None, :]) & earlier).astype(jnp.int32), 1)
    slot_ids = reach * CAP + rank_in
    picked = (slot_ids[None, :] == local_ids[:, None]).astype(jnp.int32)
    send_tok = tokens[jnp.sum(picked * local_ids[None, :], 1)]
    got_tok = []
    for reach_step in range(SPREAD):
        tok_piece = send_tok[reach_step * CAP : (reach_step + 1) * CAP]
        if reach_step > 0:
            tok_piece = from_behind(tok_piece, "dp", reach_step)
        got_tok.append(tok_piece)
    recv_tok = jnp.concatenate(got_tok, 0)
    facts = jnp.stack(
        [
            (owners * rows_dev + assign[:, 1]).astype(jnp.float32),
            lengths.astype(jnp.float32),
            group_ids.astype(jnp.float32),
            rewards,
            slot_ids.astype(jnp.float32),
        ]
    )
    facts = jnp.pad(facts, ((0, 8 - facts.shape[0]), (0, 128 - seq_dev)))[None]
    query_full, keyval_full, out_full, all_facts = gather_all((w_query, w_keyval, w_out), facts)
    query_full = query_full.reshape(-1, query_full.shape[-1])
    keyval_full = keyval_full.reshape(-1, keyval_full.shape[-1])
    out_full = out_full.reshape(-1, out_full.shape[-1])
    known = all_facts[:, :, :seq_dev].transpose(1, 0, 2).reshape(8, dp_count * seq_dev)
    seq_row = known[0].astype(jnp.int32)
    seq_len = known[1].astype(jnp.int32)
    seq_group = known[2].astype(jnp.int32)
    seq_slot = known[4].astype(jnp.int32)
    all_ids = jnp.arange(dp_count * seq_dev, dtype=jnp.int32)
    before = (seq_row[:, None] == seq_row[None, :]) & (all_ids[:, None] < all_ids[None, :])
    seq_off = jnp.sum(jnp.where(before, seq_len[:, None], 0), 0)
    member = (seq_group[None, :] == jnp.arange(groups_all, dtype=jnp.int32)[:, None]).astype(
        jnp.float32
    )
    group_mean = jnp.sum(member * known[3][None, :], 1) / jnp.maximum(jnp.sum(member, 1), 1.0)
    adv = (known[3] - jnp.sum(member * group_mean[:, None], 0)).astype(jnp.bfloat16)
    cell_ids = jnp.arange(rows_dev * ROW, dtype=jnp.int32)
    cell_row = dp_index * rows_dev + cell_ids // ROW
    inside_at = (cell_ids % ROW)[None, :] - seq_off[:, None]
    matched = (
        (seq_row[:, None] == cell_row[None, :])
        & (inside_at >= 0)
        & (inside_at < seq_len[:, None])
    )
    matched_int = matched.astype(jnp.int32)
    filled = jnp.sum(matched_int, 0) > 0
    anchor = jnp.sum(matched_int * (seq_slot[:, None] * lmax_len + inside_at), 0)
    flat_tok = recv_tok.reshape(seq_dev * lmax_len, width)
    packed = jnp.where(filled[:, None], flat_tok[anchor], jnp.zeros((), jnp.bfloat16)).reshape(
        rows_dev, ROW, width
    )
    segment = jnp.where(filled, jnp.sum(matched_int * all_ids[:, None], 0), -1).reshape(
        rows_dev, ROW
    )
    position = jnp.sum(matched_int * inside_at, 0).reshape(rows_dev, ROW)
    token_adv = jnp.sum(matched.astype(jnp.float32) * adv.astype(jnp.float32)[:, None], 0)
    token_adv = token_adv.astype(jnp.bfloat16).reshape(rows_dev, ROW)
    half = HEAD // 2
    inverse = THETA ** (-(jnp.arange(half, dtype=jnp.float32) * 2.0 / HEAD))
    angles = position.astype(jnp.float32)[..., None] * inverse
    cosine, sine = jnp.cos(angles), jnp.sin(angles)
    cosine = jnp.concatenate([cosine, cosine], -1)
    sine = jnp.concatenate([-sine, sine], -1)
    gain_row = norm_gain[0]
    per_block = 1
    block_count = rows_dev // per_block
    tick_count = block_count * sections
    share = width // sections
    last = sections - 1
    outputs = []
    moving = []
    for tick_index in range(tick_count):
        if tick_index < block_count:
            current_rows = packed[tick_index * per_block : (tick_index + 1) * per_block]
        else:
            current_rows = moving[tick_index - block_count]
        block_now = jnp.int32(tick_index % block_count)
        block_at = block_now
        segment_b = lax.dynamic_slice_in_dim(segment, block_at * per_block, per_block, 0)
        cosine_b = lax.dynamic_slice_in_dim(cosine, block_at * per_block, per_block, 0)
        sine_b = lax.dynamic_slice_in_dim(sine, block_at * per_block, per_block, 0)
        result_rows = attend_block(
            current_rows,
            segment_b,
            cosine_b,
            sine_b,
            gain_row,
            query_full,
            keyval_full,
            out_full,
        )
        holder = tick_index // block_count
        if holder < last:
            moving.append(lax.ppermute(result_rows, "section", [(holder, holder + 1)]))
        else:
            kept = result_rows[:, :, last * share :]
            for target in range(last):
                part = result_rows[:, :, target * share : (target + 1) * share]
                part = lax.ppermute(part, "section", [(last, target)])
                kept = jnp.where(section_me == target, part, kept)
            outputs.append(kept)
    hidden = jnp.concatenate(outputs, 0)
    return (hidden, token_adv)


def solution(mesh):
    placed = (
        P("dp", None, None),
        P("dp"),
        P("dp", None),
        P("dp"),
        P("dp"),
        P("section", None),
        P("section", "dp", None),
        P("section", "dp", None),
        P("section", "dp", None),
    )
    return jax.shard_map(
        body,
        mesh=mesh,
        in_specs=placed,
        out_specs=(P("dp", None, "section"), P("dp", None)),
        check_vma=False,
    )
```
